32 devices in a mesh: gx: 4 (over y, x), gy: 8 (over z, core).
Axes of the slice: x: 2, y: 2, z: 4, core: 2. Of those that a mesh axis runs over, the one named last changes fastest.
Arguments:
- adjoint_start: float32 [4, 64, 128, 256], P(None, 'gx', 'gy'), may hold values from -6 to 6
- adjoint_source: float32 [4, 64, 128, 256], P(None, 'gx', 'gy'), may hold values from -6 to 6
- background_log_viscosity: float32 [64, 128, 256], P('gx', 'gy'), may hold values from -1 to 1
- background_density: float32 [64, 128, 256], P('gx', 'gy'), may hold values from 0.5 to 1.5
- marker_weights: float32 [4, 8, 32, 256], P('gx', 'gy'), may hold values from 0.1 to 2
- block_phase: int32 [4, 8, 32], P('gx', 'gy'), may hold values from 0 to 7
- block_owner: int32 [4, 8, 32], P('gx', 'gy'), may hold values from 0 to 3, as said below
- block_column: int32 [4, 8, 32], P('gx', 'gy'), may hold values from 0 to 255
- active_blocks: int32 [4, 8], P('gx', 'gy'), may hold values from 16 to 32
- phase_log_viscosity: float32 [8], replicated, may hold values from -1.5 to 1.5
- phase_density: float32 [8], replicated, may hold values from 0.5 to 2
Outputs:
- adjoint_end: float32 [4, 64, 128, 256], P(None, 'gx', 'gy')
- density_sensitivity: float32 [64, 128, 256], P('gx', 'gy')
The draws below stay inside these ranges and needn't reach their ends.
Inputs may be any that keep to these rules, and one draw needn't show every extreme that they name: `block_owner`: among the blocks of one device at most 12 name the same owner. The first 12 blocks of every device are live and name one owner, the same for all devices of one gy index.
All inputs are finite; a program needn't handle non-finite values.
Results may differ from the reference program's by a relative error of at most 0.00009.
Values sent between devices are 32-bit elements; how exact they have to be, the bound alone decides.
A program may use at most 64 MiB of HBM per device.

```python
import math
import jax
import jax.numpy as jnp

CX = 16
CY = 16
CZ = 256
MB = 32
NPH = 8
CAP = 12
NX = 64
NY = 128
NZ = 256
N_GX = 4
N_GY = 8


def draw_block_owner(key, part):
    device_keys = jax.random.split(jax.random.fold_in(key, 11), N_GX * N_GY)
    leader = jax.random.randint(jax.random.fold_in(key, 12), (1, N_GY), 0, N_GX)
    leaders = jnp.broadcast_to(leader, (N_GX, N_GY)).reshape(-1)

    def for_device(device_key, first_owner):
        shuffled = jax.random.permutation(device_key, (N_GX - 1) * CAP)[:MB - CAP]
        others = (shuffled // CAP + first_owner + 1) % N_GX
        return jnp.concatenate([jnp.full((CAP,), first_owner, jnp.int32), others.astype(jnp.int32)])
    return jax.vmap(for_device)(device_keys, leaders).reshape(N_GX, N_GY, MB)


def draw_active_blocks(key, part):
    counted = jax.random.randint(jax.random.fold_in(key, 21), (N_GX * N_GY,), MB // 2, MB + 1)
    chosen = jax.random.randint(jax.random.fold_in(key, 22), (), 0, N_GX * N_GY)
    counted = jnp.where(jnp.arange(N_GX * N_GY) == chosen, MB, counted)
    return counted.astype(jnp.int32).reshape(N_GX, N_GY)


def with_ends(drawn, own_key, least, high):
    longest = drawn.shape.index(max(drawn.shape))
    spots = []
    for shift in (0, 1):
        where = [jax.random.randint(jax.random.fold_in(own_key, axis), (), 0, length) for axis, length in enumerate(drawn.shape)]
        where[longest] = (where[longest] + shift) % drawn.shape[longest]
        spots.append(tuple(where))
    return drawn.at[spots[0]].set(least).at[spots[1]].set(high)


def steps_of(rng, shape, cuts, least, top_value):
    loudness = 1.0
    for dim, parts in cuts:
        steps = jax.random.uniform(jax.random.fold_in(jax.random.fold_in(rng, 6), dim), (parts,), jnp.float32, least / len(cuts), top_value / len(cuts))
        loudness = loudness * jnp.repeat(jnp.exp(steps), shape[dim] // parts).reshape((-1,) + (1,) * (len(shape) - 1 - dim))
    return loudness


def bell_draw(own_key, shape, deviation, limit, pieces=(), kind=jnp.bfloat16):
    drawn = deviation * jax.random.normal(own_key, shape, jnp.float32)
    if pieces:
        drawn = drawn * steps_of(own_key, shape, pieces, -0.22, 0.18)
    return jnp.clip(drawn, -limit, limit).astype(kind)


def setup_inputs(seed: int = 0) -> dict:
    streams_of = jax.random.split(jax.random.key(seed), 12)
    adjoint_start = bell_draw(streams_of[0], (4, NX, NY, NZ), 1.0, 6.0, ((1, 4), (2, 8)), jnp.float32)
    adjoint_source = bell_draw(streams_of[1], (4, NX, NY, NZ), 1.0, 6.0, ((1, 4), (2, 8)), jnp.float32)
    background_log_viscosity = jnp.clip(jax.random.uniform(streams_of[2], (NX, NY, NZ), jnp.float32, -1.0, 1.0) * steps_of(streams_of[2], (NX, NY, NZ), ((0, 4), (1, 8)), -0.4, 0.0), -1.0, 1.0)
    background_density = jnp.clip(0.5 + 1.0 * jax.random.uniform(streams_of[3], (NX, NY, NZ), jnp.float32) ** steps_of(streams_of[3], (NX, NY, NZ), ((0, 4), (1, 8)), -0.2, 0.2), 0.5, 1.5)
    marker_weights = jnp.clip(jnp.exp(math.log(2.0) - 2.9957323 * jax.random.uniform(streams_of[4], (N_GX, N_GY, MB, CZ), jnp.float32) ** steps_of(streams_of[4], (N_GX, N_GY, MB, CZ), ((0, 4), (1, 8)), -0.2, 0.2)), 0.1, 2.0)
    block_phase = with_ends(jax.random.randint(streams_of[5], (N_GX, N_GY, MB), 0, NPH), jax.random.fold_in(streams_of[5], 1), 0, NPH - 1).astype(jnp.int32)
    block_owner = draw_block_owner(jax.random.fold_in(streams_of[11], 71), 0)
    block_column = with_ends(jax.random.randint(streams_of[7], (N_GX, N_GY, MB), 0, CX * CY), jax.random.fold_in(streams_of[7], 1), 0, (CX * CY) - 1).astype(jnp.int32)
    active_blocks = draw_active_blocks(jax.random.fold_in(streams_of[11], 71), 0)
    phase_log_viscosity = jnp.clip(jax.random.uniform(streams_of[9], (NPH,), jnp.float32, -1.5, 1.5), -1.5, 1.5)
    phase_density = jnp.clip(jax.random.uniform(streams_of[10], (NPH,), jnp.float32, 0.5, 2.0), 0.5, 2.0)
    return dict(adjoint_start=adjoint_start, adjoint_source=adjoint_source, background_log_viscosity=background_log_viscosity, background_density=background_density, marker_weights=marker_weights, block_phase=block_phase, block_owner=block_owner, block_column=block_column, active_blocks=active_blocks, phase_log_viscosity=phase_log_viscosity, phase_density=phase_density)


RELAX_VELOCITY = 0.6
RELAX_PRESSURE = 0.5


def lookup(identity, table):
    matches = identity[..., None] == jnp.arange(table.shape[0], dtype=jnp.int32)
    return jnp.sum(jnp.where(matches, table, 0.0), axis=-1)


def neighbour(padded, axis_dim, step):
    extent = [padded.shape[0] - 2, padded.shape[1] - 2, padded.shape[2] - 2]
    offset = [1, 1, 1]
    offset[axis_dim] = offset[axis_dim] + step
    return padded[offset[0]:offset[0] + extent[0], offset[1]:offset[1] + extent[1], offset[2]:offset[2] + extent[2]]


def smooth_once(field_pad, visc_pad, source):
    centre_visc = neighbour(visc_pad, 0, 0)
    upper_coef = [0.5 * (centre_visc + neighbour(visc_pad, axis_dim, 1)) for axis_dim in range(3)]
    lower_coef = [0.5 * (centre_visc + neighbour(visc_pad, axis_dim, -1)) for axis_dim in range(3)]
    diagonal = upper_coef[0] + lower_coef[0] + upper_coef[1] + lower_coef[1] + upper_coef[2] + lower_coef[2]
    pressure = field_pad[3]
    centre_press = neighbour(pressure, 0, 0)
    results = []
    divergence = jnp.zeros_like(centre_visc)
    for component in range(3):
        velocity = field_pad[component]
        centre = neighbour(velocity, 0, 0)
        viscous = jnp.zeros_like(centre)
        for axis_dim in range(3):
            viscous = viscous + upper_coef[axis_dim] * (centre - neighbour(velocity, axis_dim, 1))
            viscous = viscous + lower_coef[axis_dim] * (centre - neighbour(velocity, axis_dim, -1))
        pressure_push = neighbour(pressure, component, 1) - centre_press
        residual = source[component] - viscous - pressure_push
        results.append(centre + RELAX_VELOCITY * residual / diagonal)
        divergence = divergence + (centre - neighbour(velocity, component, -1))
    residual_press = source[3] + divergence
    results.append(centre_press - RELAX_PRESSURE * centre_visc * residual_press)
    return jnp.stack(results)


def reference(adjoint_start, adjoint_source, background_log_viscosity, background_density, marker_weights, block_phase, block_owner, block_column, active_blocks, phase_log_viscosity, phase_density):
    active = jnp.arange(MB, dtype=jnp.int32)[None, None, :] < active_blocks[:, :, None]
    weights = jnp.where(active[..., None], marker_weights, 0.0)
    log_term = weights * lookup(block_phase, phase_log_viscosity)[..., None]
    rho_term = weights * lookup(block_phase, phase_density)[..., None]
    row_index = (block_owner * CX + block_column // CY).astype(jnp.int32)
    col_index = (jnp.arange(N_GY, dtype=jnp.int32)[None, :, None] * CY + block_column % CY).astype(jnp.int32)
    empty = jnp.zeros((NX, NY, NZ), jnp.float32)
    weight_sum = 1.0 + empty.at[row_index, col_index].add(weights)
    log_sum = empty.at[row_index, col_index].add(log_term)
    density_sum = empty.at[row_index, col_index].add(rho_term)
    viscosity = jnp.exp((background_log_viscosity + log_sum) / weight_sum)
    density = (background_density + density_sum) / weight_sum
    visc_pad = jnp.pad(viscosity, 1)
    fields = adjoint_start
    for sweep_index in range(2):
        fields = smooth_once(jnp.pad(fields, ((0, 0), (1, 1), (1, 1), (1, 1))), visc_pad, adjoint_source)
    return fields, density * fields[2]
```

```python
import functools

import jax
import jax.numpy as jnp
from jax import lax
from jax.experimental import pallas as pl
from jax.experimental.pallas import tpu as pltpu
from jax.sharding import PartitionSpec as P

RELAX_VELOCITY = 0.6
RELAX_PRESSURE = 0.5
MESH = pl.DeviceIdType.MESH


def kernel(
    n,
    m,
    start_h,
    source_h,
    bglog_h,
    bgden_h,
    weights_h,
    phase_ref,
    owner_ref,
    column_ref,
    active_ref,
    table_log,
    table_den,
    out_ref,
    sens_ref,
    f0,
    f1,
    src,
    bg,
    bd,
    visc,
    dens,
    cx,
    cyu,
    cyl,
    czu,
    czl,
    rec,
    sums,
    wb,
    mraw,
    mb,
    ys,
    yr,
    ysv,
    yrv,
    ys2,
    yr2,
    local_sem,
    w_send,
    w_recv,
    m_send,
    m_recv,
    h_send,
    h_recv,
):
    X, Y, Z = bd.shape
    B = weights_h.shape[2]
    W = mraw.shape[1]
    rows = wb.shape[0]
    a = lax.axis_index("gx")
    b = lax.axis_index("gy")
    has_xlo, has_xhi = a > 0, a < n - 1
    has_ylo, has_yhi = b > 0, b < m - 1

    own_w = pltpu.make_async_copy(
        weights_h.at[0, 0], wb.at[pl.ds(pl.multiple_of(a * B, B), B)], local_sem.at[0]
    )
    own_start = pltpu.make_async_copy(start_h, f0.at[:, pl.ds(1, X)], local_sem.at[1])
    own_bg = pltpu.make_async_copy(bglog_h, bg.at[pl.ds(1, X)], local_sem.at[2])
    own_bd = pltpu.make_async_copy(bgden_h, bd, local_sem.at[3])
    own_src = pltpu.make_async_copy(source_h, src, local_sem.at[4])
    own_start.start()
    own_w.start()
    own_bg.start()
    own_bd.start()
    own_src.start()

    barrier = pltpu.get_barrier_semaphore()
    for s in range(1, n):
        pl.semaphore_signal(
            barrier, inc=1, device_id=(lax.rem(a + s, n), b), device_id_type=MESH
        )

    @pl.when(has_ylo)
    def _():
        pl.semaphore_signal(barrier, inc=1, device_id=(a, b - 1), device_id_type=MESH)

    @pl.when(has_yhi)
    def _():
        pl.semaphore_signal(barrier, inc=1, device_id=(a, b + 1), device_id_type=MESH)

    phase = phase_ref[0]
    lane = lax.broadcasted_iota(jnp.int32, (1, B), 1)
    live = lane < active_ref[0, 0]
    code = jnp.where(live, owner_ref[0] * (X * Y) + column_ref[0], -2 * X * Y)
    log_value = jnp.zeros((1, B), jnp.float32)
    den_value = jnp.zeros((1, B), jnp.float32)
    for k in range(table_log.shape[0]):
        log_value = jnp.where(phase == k, table_log[k], log_value)
        den_value = jnp.where(phase == k, table_den[k], den_value)
    mraw[...] = jnp.zeros_like(mraw)
    mraw[0:1, 0:B] = code.astype(jnp.float32)
    mraw[1:2, 0:B] = log_value
    mraw[2:3, 0:B] = den_value
    mb[0] = pltpu.roll(mraw[...], a * B, 1)

    @pl.when(a == 0)
    def _():
        f0[:, 0] = jnp.zeros((4, Y, Z), jnp.float32)
        f1[:, 0] = jnp.zeros((4, Y, Z), jnp.float32)
        bg[0] = jnp.zeros((Y, Z), jnp.float32)

    @pl.when(a == n - 1)
    def _():
        f0[:, X + 1] = jnp.zeros((4, Y, Z), jnp.float32)
        f1[:, X + 1] = jnp.zeros((4, Y, Z), jnp.float32)
        bg[X + 1] = jnp.zeros((Y, Z), jnp.float32)

    @pl.when(b == 0)
    def _():
        yr[0] = jnp.zeros((4, X, Z), jnp.float32)
        yr2[0] = jnp.zeros((4, X, Z), jnp.float32)
        yrv[0] = jnp.zeros((X, Z), jnp.float32)

    @pl.when(b == m - 1)
    def _():
        yr[1] = jnp.zeros((4, X, Z), jnp.float32)
        yr2[1] = jnp.zeros((4, X, Z), jnp.float32)
        yrv[1] = jnp.zeros((X, Z), jnp.float32)

    pl.semaphore_wait(
        barrier, n - 1 + has_ylo.astype(jnp.int32) + has_yhi.astype(jnp.int32)
    )

    def remote(source, target, slot, peer):
        return pltpu.make_async_remote_copy(
            src_ref=source,
            dst_ref=target,
            send_sem=h_send.at[slot],
            recv_sem=h_recv.at[slot],
            device_id=peer,
            device_id_type=MESH,
        )

    w_copies, m_copies = [], []
    for s in range(1, n):
        peer = (lax.rem(a + s, n), b)
        m_copies.append(
            pltpu.make_async_remote_copy(
                mb.at[0], mb.at[s], m_send.at[s], m_recv.at[s], peer, MESH
            )
        )
        w_copies.append(
            pltpu.make_async_remote_copy(
                weights_h.at[0, 0],
                wb.at[pl.ds(pl.multiple_of(a * B, B), B)],
                w_send.at[s],
                w_recv.at[s],
                peer,
                MESH,
            )
        )
        w_copies[-1].start()
        m_copies[-1].start()

    lo_x, hi_x, lo_y, hi_y = (a - 1, b), (a + 1, b), (a, b - 1), (a, b + 1)
    pairs = {
        "bg": (
            remote(bglog_h.at[0], bg.at[X + 1], 0, lo_x),
            remote(bglog_h.at[X - 1], bg.at[0], 1, hi_x),
            has_xlo,
            has_xhi,
        ),
        "x0": (
            remote(start_h.at[:, 0], f0.at[:, X + 1], 2, lo_x),
            remote(start_h.at[pl.ds(0, 3), X - 1], f0.at[pl.ds(0, 3), 0], 3, hi_x),
            has_xlo,
            has_xhi,
        ),
        "y0": (
            remote(ys.at[0], yr.at[1], 4, lo_y),
            remote(ys.at[1, pl.ds(0, 3)], yr.at[0, pl.ds(0, 3)], 5, hi_y),
            has_ylo,
            has_yhi,
        ),
        "yv": (
            remote(ysv.at[0], yrv.at[1], 6, lo_y),
            remote(ysv.at[1], yrv.at[0], 7, hi_y),
            has_ylo,
            has_yhi,
        ),
        "x1": (
            remote(f1.at[:, 1], f1.at[:, X + 1], 8, lo_x),
            remote(f1.at[pl.ds(0, 3), X], f1.at[pl.ds(0, 3), 0], 9, hi_x),
            has_xlo,
            has_xhi,
        ),
        "y1": (
            remote(ys2.at[0], yr2.at[1], 10, lo_y),
            remote(ys2.at[1, pl.ds(0, 3)], yr2.at[0, pl.ds(0, 3)], 11, hi_y),
            has_ylo,
            has_yhi,
        ),
    }

    def launch_down(name):
        down, up, lo, hi = pairs[name]
        pl.when(lo)(down.start)

    def launch_up(name):
        down, up, lo, hi = pairs[name]
        pl.when(hi)(up.start)

    def arrive(name):
        down, up, lo, hi = pairs[name]
        pl.when(hi)(down.wait_recv)
        pl.when(lo)(up.wait_recv)

    def sent(name):
        down, up, lo, hi = pairs[name]
        pl.when(lo)(down.wait_send)
        pl.when(hi)(up.wait_send)

    launch_down("bg")
    launch_up("bg")
    launch_down("x0")
    launch_up("x0")

    own_start.wait()
    for c in range(4):
        for x in range(X):
            ys[0, c, x : x + 1, :] = f0[c, x + 1, 0:1, :]
            if c < 3:
                ys[1, c, x : x + 1, :] = f0[c, x + 1, Y - 1 : Y, :]
    launch_down("y0")
    launch_up("y0")

    own_w.wait()
    own_bg.wait()
    own_bd.wait()
    for s in range(1, n):
        m_copies[s - 1].wait_recv()
        w_copies[s - 1].wait_recv()

    meta = mb[0]
    for s in range(1, n):
        meta = meta + mb[s]
    columns = meta.T
    weights = wb[...]
    payload = jnp.concatenate(
        [weights, weights * columns[:rows, 1:2], weights * columns[:rows, 2:3]], axis=1
    )
    coarse = payload.astype(jnp.bfloat16)
    fine = (payload - coarse.astype(jnp.float32)).astype(jnp.bfloat16)
    cells = (X + 2) * Y
    ids = lax.broadcasted_iota(jnp.int32, (cells, rows), 0) + (a * (X * Y) - Y)
    hot = (ids.astype(jnp.float32) == meta[0:1, :rows]).astype(jnp.float32).astype(jnp.bfloat16)
    sums[...] = jnp.dot(hot, coarse, preferred_element_type=jnp.float32) + jnp.dot(
        hot, fine, preferred_element_type=jnp.float32
    )

    arrive("bg")
    for i in range(X + 2):
        part = sums[i * Y : (i + 1) * Y, :]
        scale = 1.0 / (1.0 + part[:, :Z])
        value = jnp.exp((bg[i] + part[:, Z : 2 * Z]) * scale)
        if i == 0:
            value = jnp.where(has_xlo, value, 0.0)
        elif i == X + 1:
            value = jnp.where(has_xhi, value, 0.0)
        else:
            dens[i - 1] = (bd[i - 1] + part[:, 2 * Z :]) * scale
            ysv[0, i - 1 : i, :] = value[0:1, :]
            ysv[1, i - 1 : i, :] = value[Y - 1 : Y, :]
        visc[i] = value
    launch_down("yv")
    launch_up("yv")

    row_id = lax.broadcasted_iota(jnp.int32, (Y, Z), 0)
    lane_id = lax.broadcasted_iota(jnp.int32, (Y, Z), 1)
    first_row, last_row = row_id == 0, row_id == Y - 1
    first_lane, last_lane = lane_id == 0, lane_id == Z - 1

    def y_next(plane, halo):
        return jnp.where(last_row, halo, pltpu.roll(plane, Y - 1, 0))

    def y_prev(plane, halo):
        return jnp.where(first_row, halo, pltpu.roll(plane, 1, 0))

    def z_next(plane):
        return pltpu.roll(plane, Z - 1, 1)

    def z_prev(plane):
        return pltpu.roll(plane, 1, 1)

    for i in range(X + 1):
        cx[i] = 0.5 * (visc[i] + visc[i + 1])

    own_src.wait()
    arrive("yv")
    for x in range(X):
        v = visc[x + 1]
        half = 0.5 * v
        y_up = 0.5 * (v + y_next(v, yrv[1, x : x + 1, :]))
        y_down = 0.5 * (v + y_prev(v, yrv[0, x : x + 1, :]))
        z_up = jnp.where(last_lane, 0.0, 0.5 * (v + z_next(v)))
        z_down = z_prev(z_up)
        edge = jnp.where(first_lane | last_lane, half, 0.0)
        diagonal = cx[x] + cx[x + 1] + y_up + y_down + z_up + z_down + edge
        cyu[x] = y_up
        cyl[x] = y_down
        czu[x] = z_up
        czl[x] = z_down
        rec[x] = RELAX_VELOCITY / diagonal
    arrive("y0")
    arrive("x0")

    def sweep(field, halo, x):
        i = x + 1
        press = field[3, i]
        scale = rec[x]
        divergence = src[3, x]
        results = []
        for c in range(3):
            u = field[c, i]
            below_x = field[c, i - 1]
            below_y = y_prev(u, halo[0, c, x : x + 1, :])
            below_z = z_prev(u)
            total = cx[i] * field[c, i + 1] + cx[i - 1] * below_x
            total = total + cyu[x] * y_next(u, halo[1, c, x : x + 1, :]) + cyl[x] * below_y
            total = total + czu[x] * z_next(u) + czl[x] * below_z
            if c == 0:
                ahead, behind = field[3, i + 1], below_x
            elif c == 1:
                ahead, behind = y_next(press, halo[1, 3, x : x + 1, :]), below_y
            else:
                ahead = jnp.where(last_lane, 0.0, z_next(press))
                behind = jnp.where(first_lane, 0.0, below_z)
            residual = src[c, x] + total - (ahead - press)
            results.append((1.0 - RELAX_VELOCITY) * u + scale * residual)
            divergence = divergence + (u - behind)
        results.append(press - RELAX_PRESSURE * visc[i] * divergence)
        return results

    def first(x):
        for c, plane in enumerate(sweep(f0, yr, x)):
            f1[c, x + 1] = plane
            ys2[0, c, x : x + 1, :] = plane[0:1, :]
            if c < 3:
                ys2[1, c, x : x + 1, :] = plane[Y - 1 : Y, :]

    first(0)
    launch_down("x1")
    first(X - 1)
    launch_up("x1")
    for x in range(1, X - 1):
        first(x)
    launch_down("y1")
    launch_up("y1")
    arrive("y1")

    def second(x):
        planes = sweep(f1, yr2, x)
        for c, plane in enumerate(planes):
            out_ref[c, x] = plane
        sens_ref[x] = dens[x] * planes[2]

    for x in range(1, X - 1):
        second(x)
    arrive("x1")
    second(0)
    second(X - 1)

    for copy in w_copies + m_copies:
        copy.wait_send()
    for name in pairs:
        sent(name)


def on_device(n, m, *arrays):
    start, weights = arrays[0], arrays[4]
    _, X, Y, Z = start.shape
    B = weights.shape[2]
    rows = n * B
    W = -(-rows // 128) * 128
    f32 = jnp.float32
    vmem = pl.BlockSpec(memory_space=pltpu.VMEM)
    smem = pl.BlockSpec(memory_space=pltpu.SMEM)
    anywhere = pl.BlockSpec(memory_space=pl.ANY)
    block = pltpu.VMEM((X, Y, Z), f32)
    padded = pltpu.VMEM((X + 2, Y, Z), f32)
    faces = pltpu.VMEM((2, 4, X, Z), f32)
    face = pltpu.VMEM((2, X, Z), f32)
    dma = pltpu.SemaphoreType.DMA
    return pl.pallas_call(
        functools.partial(kernel, n, m),
        out_shape=(
            jax.ShapeDtypeStruct((4, X, Y, Z), f32),
            jax.ShapeDtypeStruct((X, Y, Z), f32),
        ),
        in_specs=[anywhere] * 5 + [vmem] * 3 + [smem] * 3,
        out_specs=(vmem, vmem),
        scratch_shapes=[
            pltpu.VMEM((4, X + 2, Y, Z), f32),
            pltpu.VMEM((4, X + 2, Y, Z), f32),
            pltpu.VMEM((4, X, Y, Z), f32),
            padded,
            block,
            padded,
            block,
            pltpu.VMEM((X + 1, Y, Z), f32),
            block,
            block,
            block,
            block,
            block,
            pltpu.VMEM(((X + 2) * Y, 3 * Z), f32),
            pltpu.VMEM((rows, Z), f32),
            pltpu.VMEM((8, W), f32),
            pltpu.VMEM((n, 8, W), f32),
            faces,
            faces,
            face,
            face,
            faces,
            faces,
            dma((5,)),
            dma((n,)),
            dma((n,)),
            dma((n,)),
            dma((n,)),
            dma((12,)),
            dma((12,)),
        ],
        compiler_params=pltpu.CompilerParams(
            collective_id=0, has_side_effects=True, vmem_limit_bytes=40 * 1024 * 1024
        ),
    )(*arrays)


def solution(mesh):
    in_specs = (
        P(None, "gx", "gy", None),
        P(None, "gx", "gy", None),
        P("gx", "gy", None),
        P("gx", "gy", None),
        P("gx", "gy", None, None),
        P("gx", "gy", None),
        P("gx", "gy", None),
        P("gx", "gy", None),
        P("gx", "gy"),
        P(),
        P(),
    )
    out_specs = (P(None, "gx", "gy", None), P("gx", "gy", None))
    return jax.shard_map(
        functools.partial(on_device, mesh.shape["gx"], mesh.shape["gy"]),
        mesh=mesh,
        in_specs=in_specs,
        out_specs=out_specs,
        check_vma=False,
    )
```

```python
import functools

import jax
import jax.numpy as jnp
from jax import lax
from jax.experimental import pallas as pl
from jax.experimental.pallas import tpu as pltpu
from jax.sharding import PartitionSpec as P

RELAX_VELOCITY = 0.6
RELAX_PRESSURE = 0.5
MESH = pl.DeviceIdType.MESH


def kernel(
    n,
    m,
    start_h,
    source_h,
    bglog_h,
    bgden_h,
    weights_h,
    phase_h,
    owner_h,
    column_h,
    active_ref,
    table_log_h,
    table_den_h,
    out_ref,
    sens_ref,
    f0,
    f1,
    src,
    bg,
    bd,
    visc,
    dens,
    cx,
    cyu,
    cyl,
    czu,
    czl,
    rec,
    sums,
    wb,
    mraw,
    mb,
    ys,
    yr,
    ysv,
    yrv,
    ys2,
    yr2,
    fin,
    fin2,
    fsrc,
    vin,
    fc,
    xs,
    xrs,
    xr,
    phase_ref,
    owner_ref,
    column_ref,
    table_log,
    table_den,
    local_sem,
    w_send,
    w_recv,
    m_send,
    m_recv,
    h_send,
    h_recv,
):
    X, Y, Z = bd.shape
    B = weights_h.shape[2]
    W = mraw.shape[1]
    rows = wb.shape[0]
    a = lax.axis_index("gx")
    b = lax.axis_index("gy")
    has_xlo, has_xhi = a > 0, a < n - 1
    has_ylo, has_yhi = b > 0, b < m - 1

    barrier = pltpu.get_barrier_semaphore()
    for s in range(1, n):
        pl.semaphore_signal(
            barrier, inc=1, device_id=(lax.rem(a + s, n), b), device_id_type=MESH
        )

    @pl.when(has_ylo)
    def _():
        pl.semaphore_signal(barrier, inc=1, device_id=(a, b - 1), device_id_type=MESH)

    @pl.when(has_yhi)
    def _():
        pl.semaphore_signal(barrier, inc=1, device_id=(a, b + 1), device_id_type=MESH)

    small = [
        pltpu.make_async_copy(source, target, local_sem.at[5 + k])
        for k, (source, target) in enumerate(
            [
                (phase_h, phase_ref),
                (owner_h, owner_ref),
                (column_h, column_ref),
                (table_log_h, table_log),
                (table_den_h, table_den),
            ]
        )
    ]
    for copy in small:
        copy.start()
    own_w = pltpu.make_async_copy(
        weights_h.at[0, 0], wb.at[pl.ds(pl.multiple_of(a * B, B), B)], local_sem.at[0]
    )
    own_start = pltpu.make_async_copy(start_h, f0.at[:, pl.ds(1, X)], local_sem.at[1])
    own_bg = pltpu.make_async_copy(bglog_h, bg.at[pl.ds(1, X)], local_sem.at[2])
    own_bd = pltpu.make_async_copy(bgden_h, bd, local_sem.at[3])
    own_src = pltpu.make_async_copy(source_h, src, local_sem.at[4])
    own_start.start()
    own_w.start()
    own_bg.start()
    own_bd.start()
    own_src.start()

    for copy in small:
        copy.wait()

    phase = phase_ref[0]
    lane = lax.broadcasted_iota(jnp.int32, (1, B), 1)
    live = lane < active_ref[0, 0]
    code = jnp.where(live, owner_ref[0] * (X * Y) + column_ref[0], -2 * X * Y)
    log_value = jnp.zeros((1, B), jnp.float32)
    den_value = jnp.zeros((1, B), jnp.float32)
    for k in range(table_log.shape[0]):
        log_value = jnp.where(phase == k, table_log[k], log_value)
        den_value = jnp.where(phase == k, table_den[k], den_value)
    mraw[...] = jnp.zeros_like(mraw)
    mraw[0:1, 0:B] = code.astype(jnp.float32)
    mraw[1:2, 0:B] = log_value
    mraw[2:3, 0:B] = den_value
    mb[0] = pltpu.roll(mraw[...], a * B, 1)

    @pl.when(a == 0)
    def _():
        f0[:, 0] = jnp.zeros((4, Y, Z), jnp.float32)
        f1[:, 0] = jnp.zeros((4, Y, Z), jnp.float32)
        bg[0] = jnp.zeros((Y, Z), jnp.float32)
        xr[0] = jnp.zeros((8, Z), jnp.float32)

    @pl.when(a == n - 1)
    def _():
        f0[:, X + 1] = jnp.zeros((4, Y, Z), jnp.float32)
        f1[:, X + 1] = jnp.zeros((4, Y, Z), jnp.float32)
        bg[X + 1] = jnp.zeros((Y, Z), jnp.float32)
        xr[1] = jnp.zeros((8, Z), jnp.float32)

    @pl.when(b == 0)
    def _():
        yr[0] = jnp.zeros((4, X, Z), jnp.float32)
        yr2[0] = jnp.zeros((4, X, Z), jnp.float32)
        yrv[0] = jnp.zeros((X, Z), jnp.float32)

    @pl.when(b == m - 1)
    def _():
        yr[1] = jnp.zeros((4, X, Z), jnp.float32)
        yr2[1] = jnp.zeros((4, X, Z), jnp.float32)
        yrv[1] = jnp.zeros((X, Z), jnp.float32)

    pl.semaphore_wait(
        barrier, n - 1 + has_ylo.astype(jnp.int32) + has_yhi.astype(jnp.int32)
    )

    def remote(source, target, slot, peer):
        return pltpu.make_async_remote_copy(
            src_ref=source,
            dst_ref=target,
            send_sem=h_send.at[slot],
            recv_sem=h_recv.at[slot],
            device_id=peer,
            device_id_type=MESH,
        )

    w_copies, m_copies = [], []
    for s in range(1, n):
        peer = (lax.rem(a + s, n), b)
        m_copies.append(
            pltpu.make_async_remote_copy(
                mb.at[0], mb.at[s], m_send.at[s], m_recv.at[s], peer, MESH
            )
        )
        w_copies.append(
            pltpu.make_async_remote_copy(
                weights_h.at[0, 0],
                wb.at[pl.ds(pl.multiple_of(a * B, B), B)],
                w_send.at[s],
                w_recv.at[s],
                peer,
                MESH,
            )
        )
        w_copies[-1].start()
        m_copies[-1].start()

    lo_x, hi_x, lo_y, hi_y = (a - 1, b), (a + 1, b), (a, b - 1), (a, b + 1)
    pairs = {
        "bg": (
            remote(bglog_h.at[0], bg.at[X + 1], 0, lo_x),
            remote(bglog_h.at[X - 1], bg.at[0], 1, hi_x),
            has_xlo,
            has_xhi,
        ),
        "x0": (
            remote(start_h.at[:, 0], f0.at[:, X + 1], 2, lo_x),
            remote(start_h.at[pl.ds(0, 3), X - 1], f0.at[pl.ds(0, 3), 0], 3, hi_x),
            has_xlo,
            has_xhi,
        ),
        "y0": (
            remote(ys.at[0], yr.at[1], 4, lo_y),
            remote(ys.at[1, pl.ds(0, 3)], yr.at[0, pl.ds(0, 3)], 5, hi_y),
            has_ylo,
            has_yhi,
        ),
        "yv": (
            remote(ysv.at[0], yrv.at[1], 6, lo_y),
            remote(ysv.at[1], yrv.at[0], 7, hi_y),
            has_ylo,
            has_yhi,
        ),
        "x1": (
            remote(xs.at[0], f1.at[:, X + 1], 8, lo_x),
            remote(xs.at[1, pl.ds(0, 3)], f1.at[pl.ds(0, 3), 0], 9, hi_x),
            has_xlo,
            has_xhi,
        ),
        "y1": (
            remote(ys2.at[0], yr2.at[1], 10, lo_y),
            remote(ys2.at[1, pl.ds(0, 3)], yr2.at[0, pl.ds(0, 3)], 11, hi_y),
            has_ylo,
            has_yhi,
        ),
    }

    pairs["xr"] = (
        remote(xrs.at[0], xr.at[1], 12, lo_x),
        remote(xrs.at[1], xr.at[0], 13, hi_x),
        has_xlo,
        has_xhi,
    )

    def launch_down(name):
        down, up, lo, hi = pairs[name]
        pl.when(lo)(down.start)

    def launch_up(name):
        down, up, lo, hi = pairs[name]
        pl.when(hi)(up.start)

    def arrive(name):
        down, up, lo, hi = pairs[name]
        pl.when(hi)(down.wait_recv)
        pl.when(lo)(up.wait_recv)

    def sent(name):
        down, up, lo, hi = pairs[name]
        pl.when(lo)(down.wait_send)
        pl.when(hi)(up.wait_send)

    launch_down("bg")
    launch_up("bg")
    launch_down("x0")
    launch_up("x0")

    own_start.wait()
    for c in range(4):
        for x in range(X):
            ys[0, c, x : x + 1, :] = f0[c, x + 1, 0:1, :]
            if c < 3:
                ys[1, c, x : x + 1, :] = f0[c, x + 1, Y - 1 : Y, :]
    launch_down("y0")
    launch_up("y0")
    edges = (0, Y - 1)
    inners = (1, Y - 2)
    for side in range(2):
        for c in range(4):
            for x in range(X):
                fin[side, c, x : x + 1, :] = f0[c, x + 1, inners[side] : inners[side] + 1, :]
                if side == 1 and c == 3:
                    ys[1, c, x : x + 1, :] = f0[c, x + 1, Y - 1 : Y, :]
    own_src.wait()
    for side in range(2):
        for c in range(4):
            for x in range(X):
                fsrc[side, c, x : x + 1, :] = src[c, x, edges[side] : edges[side] + 1, :]

    own_w.wait()
    own_bg.wait()
    own_bd.wait()
    for s in range(1, n):
        m_copies[s - 1].wait_recv()
        w_copies[s - 1].wait_recv()

    meta = mb[0]
    for s in range(1, n):
        meta = meta + mb[s]
    columns = meta.T
    weights = wb[...]
    payload = jnp.concatenate(
        [weights, weights * columns[:rows, 1:2], weights * columns[:rows, 2:3]], axis=1
    )
    coarse = payload.astype(jnp.bfloat16)
    fine = (payload - coarse.astype(jnp.float32)).astype(jnp.bfloat16)
    cells = (X + 2) * Y
    ids = lax.broadcasted_iota(jnp.int32, (cells, rows), 0) + (a * (X * Y) - Y)
    hot = (ids.astype(jnp.float32) == meta[0:1, :rows]).astype(jnp.float32).astype(jnp.bfloat16)
    sums[...] = jnp.dot(hot, coarse, preferred_element_type=jnp.float32) + jnp.dot(
        hot, fine, preferred_element_type=jnp.float32
    )

    arrive("bg")
    for i in range(X + 2):
        part = sums[i * Y : (i + 1) * Y, :]
        scale = 1.0 / (1.0 + part[:, :Z])
        value = jnp.exp((bg[i] + part[:, Z : 2 * Z]) * scale)
        if i == 0:
            value = jnp.where(has_xlo, value, 0.0)
        elif i == X + 1:
            value = jnp.where(has_xhi, value, 0.0)
        else:
            dens[i - 1] = (bd[i - 1] + part[:, 2 * Z :]) * scale
            ysv[0, i - 1 : i, :] = value[0:1, :]
            ysv[1, i - 1 : i, :] = value[Y - 1 : Y, :]
            vin[0, i - 1 : i, :] = value[1:2, :]
            vin[1, i - 1 : i, :] = value[Y - 2 : Y - 1, :]
        visc[i] = value
    launch_down("yv")
    launch_up("yv")

    row_id = lax.broadcasted_iota(jnp.int32, (X, Z), 0)
    lane_id = lax.broadcasted_iota(jnp.int32, (1, Z), 1)
    first_row, last_row = row_id == 0, row_id == X - 1
    first_lane, last_lane = lane_id == 0, lane_id == Z - 1

    def y_next(plane):
        return pltpu.roll(plane, Y - 1, 0)

    def y_prev(plane):
        return pltpu.roll(plane, 1, 0)

    def x_next(plane, halo):
        return jnp.where(last_row, halo, pltpu.roll(plane, X - 1, 0))

    def x_prev(plane, halo):
        return jnp.where(first_row, halo, pltpu.roll(plane, 1, 0))

    def z_next(plane):
        return pltpu.roll(plane, Z - 1, 1)

    def z_prev(plane):
        return pltpu.roll(plane, 1, 1)

    def z_coefs(v):
        z_up = jnp.where(last_lane, 0.0, 0.5 * (v + z_next(v)))
        edge = jnp.where(first_lane | last_lane, 0.5 * v, 0.0)
        return z_up, z_prev(z_up), edge

    def update(coefs, scale, source, value, nexts, prevs, v):
        press = value[3]
        divergence = source[3]
        results = []
        for c in range(3):
            u = value[c]
            above = [nexts(c, d) for d in range(3)]
            below = [prevs(c, d) for d in range(3)]
            total = coefs[0] * above[0] + coefs[1] * below[0]
            total = total + coefs[2] * above[1] + coefs[3] * below[1]
            total = total + coefs[4] * above[2] + coefs[5] * below[2]
            ahead, behind = nexts(3, c), below[c]
            if c == 2:
                ahead = jnp.where(last_lane, 0.0, ahead)
                behind = jnp.where(first_lane, 0.0, behind)
            residual = source[c] + total - (ahead - press)
            results.append((1.0 - RELAX_VELOCITY) * u + scale * residual)
            divergence = divergence + (u - behind)
        results.append(press - RELAX_PRESSURE * v * divergence)
        return results

    def sweep(field, x):
        i = x + 1
        value = [field[c, i] for c in range(4)]

        def nexts(c, d):
            return (lambda: field[c, i + 1], lambda: y_next(value[c]), lambda: z_next(value[c]))[d]()

        def prevs(c, d):
            return (lambda: field[c, i - 1], lambda: y_prev(value[c]), lambda: z_prev(value[c]))[d]()

        coefs = (cx[i], cx[i - 1], cyu[x], cyl[x], czu[x], czl[x])
        source = [src[c, x] for c in range(4)]
        return update(coefs, rec[x], source, value, nexts, prevs, visc[i])

    def face_sweep(side, field, inner, outer, low_row, high_row):
        value = [field[side, c] for c in range(4)]

        def nexts(c, d):
            if d == 0:
                return x_next(value[c], high_row(c))
            if d == 1:
                return (inner if side == 0 else outer)[side, c]
            return z_next(value[c])

        def prevs(c, d):
            if d == 0:
                return x_prev(value[c], low_row(c))
            if d == 1:
                return (outer if side == 0 else inner)[side, c]
            return z_prev(value[c])

        coefs = [fc[side, k] for k in range(6)]
        source = [fsrc[side, c] for c in range(4)]
        return update(coefs, fc[side, 6], source, value, nexts, prevs, ysv[side])

    for i in range(X + 1):
        cx[i] = 0.5 * (visc[i] + visc[i + 1])
    arrive("x0")

    def first(x):
        v = visc[x + 1]
        y_up = 0.5 * (v + y_next(v))
        y_down = 0.5 * (v + y_prev(v))
        z_up, z_down, edge = z_coefs(v)
        cyu[x] = y_up
        cyl[x] = y_down
        czu[x] = z_up
        czl[x] = z_down
        rec[x] = RELAX_VELOCITY / (cx[x] + cx[x + 1] + y_up + y_down + z_up + z_down + edge)
        for c, plane in enumerate(sweep(f0, x)):
            f1[c, x + 1] = plane
            if x == 0:
                xs[0, c] = plane
            if x == X - 1:
                xs[1, c] = plane
            for side in range(2):
                row = inners[side]
                fin2[side, c, x : x + 1, :] = plane[row : row + 1, :]

    first(0)
    launch_down("x1")
    first(X - 1)
    launch_up("x1")
    for x in range(1, X - 1):
        first(x)

    arrive("y0")
    arrive("yv")
    for side in range(2):
        y = edges[side]
        v = ysv[side]
        above, below = (vin, yrv) if side == 0 else (yrv, vin)
        x_up = 0.5 * (v + x_next(v, visc[X + 1, y : y + 1, :]))
        x_down = 0.5 * (v + x_prev(v, visc[0, y : y + 1, :]))
        y_up = 0.5 * (v + above[side])
        y_down = 0.5 * (v + below[side])
        z_up, z_down, edge = z_coefs(v)
        total = x_up + x_down + y_up + y_down + z_up + z_down + edge
        for k, coef in enumerate((x_up, x_down, y_up, y_down, z_up, z_down)):
            fc[side, k] = coef
        fc[side, 6] = RELAX_VELOCITY / total
        planes = face_sweep(
            side,
            ys,
            fin,
            yr,
            lambda c: f0[c, 0, y : y + 1, :],
            lambda c: f0[c, X + 1, y : y + 1, :],
        )
        for c, plane in enumerate(planes):
            ys2[side, c] = plane
            xrs[0, side * 4 + c : side * 4 + c + 1, :] = plane[0:1, :]
            xrs[1, side * 4 + c : side * 4 + c + 1, :] = plane[X - 1 : X, :]
        if side == 0:
            launch_down("y1")
        else:
            launch_up("y1")
            launch_down("xr")
            launch_up("xr")
    for side in range(2):
        y = edges[side]
        for c in range(4):
            for x in range(X):
                f1[c, x + 1, y : y + 1, :] = ys2[side, c, x : x + 1, :]

    def second(x):
        planes = sweep(f1, x)
        for c, plane in enumerate(planes):
            out_ref[c, x] = plane
        sens_ref[x] = dens[x] * planes[2]

    for x in range(1, X - 1):
        second(x)
    arrive("x1")
    second(0)
    second(X - 1)

    arrive("y1")
    arrive("xr")
    for side in range(2):
        y = edges[side]
        planes = face_sweep(
            side,
            ys2,
            fin2,
            yr2,
            lambda c: xr[0, side * 4 + c : side * 4 + c + 1, :],
            lambda c: xr[1, side * 4 + c : side * 4 + c + 1, :],
        )
        for x in range(X):
            for c, plane in enumerate(planes):
                out_ref[c, x, y : y + 1, :] = plane[x : x + 1, :]
            sens_ref[x, y : y + 1, :] = dens[x, y : y + 1, :] * planes[2][x : x + 1, :]

    for copy in w_copies + m_copies:
        copy.wait_send()
    for name in pairs:
        sent(name)


def flush(end, sens, end_h, sens_h, sem):
    copies = [
        pltpu.make_async_copy(end.at[c], end_h.at[c], sem.at[c]) for c in range(end.shape[0])
    ]
    copies.append(pltpu.make_async_copy(sens, sens_h, sem.at[end.shape[0]]))
    for copy in copies:
        copy.start()
    for copy in copies:
        copy.wait()


def on_device(n, m, *arrays):
    start, weights = arrays[0], arrays[4]
    _, X, Y, Z = start.shape
    B = weights.shape[2]
    rows = n * B
    W = -(-rows // 128) * 128
    f32 = jnp.float32
    vmem = pl.BlockSpec(memory_space=pltpu.VMEM)
    hbm = pl.BlockSpec(memory_space=pltpu.HBM)
    block = pltpu.VMEM((X, Y, Z), f32)
    padded = pltpu.VMEM((X + 2, Y, Z), f32)
    faces = pltpu.VMEM((2, 4, X, Z), f32)
    face = pltpu.VMEM((2, X, Z), f32)
    dma = pltpu.SemaphoreType.DMA
    pinned = [
        array if array.ndim == 2 else pltpu.with_memory_space_constraint(array, pltpu.HBM)
        for array in arrays
    ]
    end, sens = pl.pallas_call(
        functools.partial(kernel, n, m),
        out_shape=(
            jax.ShapeDtypeStruct((4, X, Y, Z), f32),
            jax.ShapeDtypeStruct((X, Y, Z), f32),
        ),
        in_specs=[hbm] * 8 + [pl.BlockSpec(memory_space=pltpu.SMEM)] + [hbm] * 2,
        out_specs=(vmem, vmem),
        scratch_shapes=[
            pltpu.VMEM((4, X + 2, Y, Z), f32),
            pltpu.VMEM((4, X + 2, Y, Z), f32),
            pltpu.VMEM((4, X, Y, Z), f32),
            padded,
            block,
            padded,
            block,
            pltpu.VMEM((X + 1, Y, Z), f32),
            block,
            block,
            block,
            block,
            block,
            pltpu.VMEM(((X + 2) * Y, 3 * Z), f32),
            pltpu.VMEM((rows, Z), f32),
            pltpu.VMEM((8, W), f32),
            pltpu.VMEM((n, 8, W), f32),
            faces,
            faces,
            face,
            face,
            faces,
            faces,
            faces,
            faces,
            faces,
            face,
            pltpu.VMEM((2, 7, X, Z), f32),
            pltpu.VMEM((2, 4, Y, Z), f32),
            pltpu.VMEM((2, 8, Z), f32),
            pltpu.VMEM((2, 8, Z), f32),
            pltpu.VMEM((1, 1, B), jnp.int32),
            pltpu.VMEM((1, 1, B), jnp.int32),
            pltpu.VMEM((1, 1, B), jnp.int32),
            pltpu.SMEM(arrays[9].shape, f32),
            pltpu.SMEM(arrays[10].shape, f32),
            dma((10,)),
            dma((n,)),
            dma((n,)),
            dma((n,)),
            dma((n,)),
            dma((14,)),
            dma((14,)),
        ],
        compiler_params=pltpu.CompilerParams(
            collective_id=0, has_side_effects=True, vmem_limit_bytes=40 * 1024 * 1024
        ),
    )(*pinned)
    return pl.pallas_call(
        flush,
        out_shape=(
            jax.ShapeDtypeStruct(end.shape, f32),
            jax.ShapeDtypeStruct(sens.shape, f32),
        ),
        in_specs=[pl.BlockSpec(memory_space=pl.ANY)] * 2,
        out_specs=(hbm, hbm),
        compiler_params=pltpu.CompilerParams(vmem_limit_bytes=1024 * 1024),
        scratch_shapes=[dma((5,))],
    )(end, sens)


def solution(mesh):
    in_specs = (
        P(None, "gx", "gy", None),
        P(None, "gx", "gy", None),
        P("gx", "gy", None),
        P("gx", "gy", None),
        P("gx", "gy", None, None),
        P("gx", "gy", None),
        P("gx", "gy", None),
        P("gx", "gy", None),
        P("gx", "gy"),
        P(),
        P(),
    )
    out_specs = (P(None, "gx", "gy", None), P("gx", "gy", None))
    return jax.shard_map(
        functools.partial(on_device, mesh.shape["gx"], mesh.shape["gy"]),
        mesh=mesh,
        in_specs=in_specs,
        out_specs=out_specs,
        check_vma=False,
    )
```

```python
import functools

import jax
import jax.numpy as jnp
from jax import lax
from jax.experimental import pallas as pl
from jax.experimental.pallas import tpu as pltpu
from jax.sharding import PartitionSpec as P

RELAX_VELOCITY = 0.6
RELAX_PRESSURE = 0.5
MESH = pl.DeviceIdType.MESH


def kernel(
    n,
    m,
    start_h,
    source_h,
    bglog_h,
    bgden_h,
    weights_h,
    phase_h,
    owner_h,
    column_h,
    active_ref,
    table_log_h,
    table_den_h,
    out_ref,
    sens_ref,
    f0,
    f1,
    src,
    bg,
    bd,
    visc,
    dens,
    cx,
    cyu,
    cyl,
    czu,
    czl,
    rec,
    sums,
    wb,
    mraw,
    mb,
    ys,
    yr,
    ysv,
    yrv,
    ys2,
    yr2,
    fin,
    fin2,
    fsrc,
    vin,
    fc,
    xs,
    xrs,
    xr,
    phase_ref,
    owner_ref,
    column_ref,
    table_log,
    table_den,
    local_sem,
    w_send,
    w_recv,
    m_send,
    m_recv,
    h_send,
    h_recv,
):
    X, Y, Z = bd.shape
    B = weights_h.shape[2]
    W = mraw.shape[1]
    rows = wb.shape[0]
    a = lax.axis_index("gx")
    b = lax.axis_index("gy")
    has_xlo, has_xhi = a > 0, a < n - 1
    has_ylo, has_yhi = b > 0, b < m - 1

    barrier = pltpu.get_barrier_semaphore()
    for s in range(1, n):
        pl.semaphore_signal(
            barrier, inc=1, device_id=(lax.rem(a + s, n), b), device_id_type=MESH
        )

    @pl.when(has_ylo)
    def _():
        pl.semaphore_signal(barrier, inc=1, device_id=(a, b - 1), device_id_type=MESH)

    @pl.when(has_yhi)
    def _():
        pl.semaphore_signal(barrier, inc=1, device_id=(a, b + 1), device_id_type=MESH)

    small = [
        pltpu.make_async_copy(source, target, local_sem.at[5 + k])
        for k, (source, target) in enumerate(
            [
                (phase_h, phase_ref),
                (owner_h, owner_ref),
                (column_h, column_ref),
                (table_log_h, table_log),
                (table_den_h, table_den),
            ]
        )
    ]
    for copy in small:
        copy.start()
    own_w = pltpu.make_async_copy(
        weights_h.at[0, 0], wb.at[pl.ds(pl.multiple_of(a * B, B), B)], local_sem.at[0]
    )
    own_start = pltpu.make_async_copy(start_h, f0.at[:, pl.ds(1, X)], local_sem.at[1])
    own_bg = pltpu.make_async_copy(bglog_h, bg.at[pl.ds(1, X)], local_sem.at[2])
    own_bd = pltpu.make_async_copy(bgden_h, bd, local_sem.at[3])
    own_src = pltpu.make_async_copy(source_h, src, local_sem.at[4])
    own_start.start()
    own_w.start()
    own_bg.start()
    own_bd.start()
    own_src.start()

    for copy in small:
        copy.wait()

    phase = phase_ref[0]
    lane = lax.broadcasted_iota(jnp.int32, (1, B), 1)
    live = lane < active_ref[0, 0]
    code = jnp.where(live, owner_ref[0] * (X * Y) + column_ref[0], -2 * X * Y)
    log_value = jnp.zeros((1, B), jnp.float32)
    den_value = jnp.zeros((1, B), jnp.float32)
    for k in range(table_log.shape[0]):
        log_value = jnp.where(phase == k, table_log[k], log_value)
        den_value = jnp.where(phase == k, table_den[k], den_value)
    mraw[...] = jnp.zeros_like(mraw)
    mraw[0:1, 0:B] = code.astype(jnp.float32)
    mraw[1:2, 0:B] = log_value
    mraw[2:3, 0:B] = den_value
    mb[0] = pltpu.roll(mraw[...], a * B, 1)

    @pl.when(a == 0)
    def _():
        f0[:, 0] = jnp.zeros((4, Y, Z), jnp.float32)
        f1[:, 0] = jnp.zeros((4, Y, Z), jnp.float32)
        bg[0] = jnp.zeros((Y, Z), jnp.float32)
        xr[0] = jnp.zeros((8, Z), jnp.float32)

    @pl.when(a == n - 1)
    def _():
        f0[:, X + 1] = jnp.zeros((4, Y, Z), jnp.float32)
        f1[:, X + 1] = jnp.zeros((4, Y, Z), jnp.float32)
        bg[X + 1] = jnp.zeros((Y, Z), jnp.float32)
        xr[1] = jnp.zeros((8, Z), jnp.float32)

    @pl.when(b == 0)
    def _():
        yr[0] = jnp.zeros((4, X, Z), jnp.float32)
        yr2[0] = jnp.zeros((4, X, Z), jnp.float32)
        yrv[0] = jnp.zeros((X, Z), jnp.float32)

    @pl.when(b == m - 1)
    def _():
        yr[1] = jnp.zeros((4, X, Z), jnp.float32)
        yr2[1] = jnp.zeros((4, X, Z), jnp.float32)
        yrv[1] = jnp.zeros((X, Z), jnp.float32)

    pl.semaphore_wait(
        barrier, n - 1 + has_ylo.astype(jnp.int32) + has_yhi.astype(jnp.int32)
    )

    def remote(source, target, slot, peer):
        return pltpu.make_async_remote_copy(
            src_ref=source,
            dst_ref=target,
            send_sem=h_send.at[slot],
            recv_sem=h_recv.at[slot],
            device_id=peer,
            device_id_type=MESH,
        )

    w_copies, m_copies = [], []
    for s in range(1, n):
        peer = (lax.rem(a + s, n), b)
        m_copies.append(
            pltpu.make_async_remote_copy(
                mb.at[0], mb.at[s], m_send.at[s], m_recv.at[s], peer, MESH
            )
        )
        w_copies.append(
            pltpu.make_async_remote_copy(
                weights_h.at[0, 0],
                wb.at[pl.ds(pl.multiple_of(a * B, B), B)],
                w_send.at[s],
                w_recv.at[s],
                peer,
                MESH,
            )
        )
        w_copies[-1].start()
        m_copies[-1].start()

    lo_x, hi_x, lo_y, hi_y = (a - 1, b), (a + 1, b), (a, b - 1), (a, b + 1)
    pairs = {
        "bg": (
            remote(bglog_h.at[0], bg.at[X + 1], 0, lo_x),
            remote(bglog_h.at[X - 1], bg.at[0], 1, hi_x),
            has_xlo,
            has_xhi,
        ),
        "x0": (
            remote(start_h.at[:, 0], f0.at[:, X + 1], 2, lo_x),
            remote(start_h.at[pl.ds(0, 3), X - 1], f0.at[pl.ds(0, 3), 0], 3, hi_x),
            has_xlo,
            has_xhi,
        ),
        "y0": (
            remote(ys.at[0], yr.at[1], 4, lo_y),
            remote(ys.at[1, pl.ds(0, 3)], yr.at[0, pl.ds(0, 3)], 5, hi_y),
            has_ylo,
            has_yhi,
        ),
        "yv": (
            remote(ysv.at[0], yrv.at[1], 6, lo_y),
            remote(ysv.at[1], yrv.at[0], 7, hi_y),
            has_ylo,
            has_yhi,
        ),
        "x1": (
            remote(xs.at[0], f1.at[:, X + 1], 8, lo_x),
            remote(xs.at[1, pl.ds(0, 3)], f1.at[pl.ds(0, 3), 0], 9, hi_x),
            has_xlo,
            has_xhi,
        ),
        "y1": (
            remote(ys2.at[0], yr2.at[1], 10, lo_y),
            remote(ys2.at[1, pl.ds(0, 3)], yr2.at[0, pl.ds(0, 3)], 11, hi_y),
            has_ylo,
            has_yhi,
        ),
    }

    pairs["xr"] = (
        remote(xrs.at[0], xr.at[1], 12, lo_x),
        remote(xrs.at[1], xr.at[0], 13, hi_x),
        has_xlo,
        has_xhi,
    )

    def launch_down(name):
        down, up, lo, hi = pairs[name]
        pl.when(lo)(down.start)

    def launch_up(name):
        down, up, lo, hi = pairs[name]
        pl.when(hi)(up.start)

    def arrive(name):
        down, up, lo, hi = pairs[name]
        pl.when(hi)(down.wait_recv)
        pl.when(lo)(up.wait_recv)

    def sent(name):
        down, up, lo, hi = pairs[name]
        pl.when(lo)(down.wait_send)
        pl.when(hi)(up.wait_send)

    launch_down("bg")
    launch_up("bg")

    own_start.wait()
    for c in range(4):
        for x in range(X):
            ys[0, c, x : x + 1, :] = f0[c, x + 1, 0:1, :]
            if c < 3:
                ys[1, c, x : x + 1, :] = f0[c, x + 1, Y - 1 : Y, :]
    launch_down("y0")
    launch_up("y0")
    edges = (0, Y - 1)
    inners = (1, Y - 2)
    for side in range(2):
        for c in range(4):
            for x in range(X):
                fin[side, c, x : x + 1, :] = f0[c, x + 1, inners[side] : inners[side] + 1, :]
                if side == 1 and c == 3:
                    ys[1, c, x : x + 1, :] = f0[c, x + 1, Y - 1 : Y, :]
    own_src.wait()
    for side in range(2):
        for c in range(4):
            for x in range(X):
                fsrc[side, c, x : x + 1, :] = src[c, x, edges[side] : edges[side] + 1, :]

    launch_down("x0")
    launch_up("x0")

    own_w.wait()
    own_bg.wait()
    own_bd.wait()
    for s in range(1, n):
        m_copies[s - 1].wait_recv()
        w_copies[s - 1].wait_recv()

    meta = mb[0]
    for s in range(1, n):
        meta = meta + mb[s]
    columns = meta.T
    weights = wb[...]
    payload = jnp.concatenate(
        [weights, weights * columns[:rows, 1:2], weights * columns[:rows, 2:3]], axis=1
    )
    coarse = payload.astype(jnp.bfloat16)
    fine = (payload - coarse.astype(jnp.float32)).astype(jnp.bfloat16)
    cells = (X + 2) * Y
    ids = lax.broadcasted_iota(jnp.int32, (cells, rows), 0) + (a * (X * Y) - Y)
    hot = (ids.astype(jnp.float32) == meta[0:1, :rows]).astype(jnp.float32).astype(jnp.bfloat16)
    sums[...] = jnp.dot(hot, coarse, preferred_element_type=jnp.float32) + jnp.dot(
        hot, fine, preferred_element_type=jnp.float32
    )

    arrive("bg")
    for i in range(X + 2):
        part = sums[i * Y : (i + 1) * Y, :]
        scale = 1.0 / (1.0 + part[:, :Z])
        value = jnp.exp((bg[i] + part[:, Z : 2 * Z]) * scale)
        if i == 0:
            value = jnp.where(has_xlo, value, 0.0)
        elif i == X + 1:
            value = jnp.where(has_xhi, value, 0.0)
        else:
            dens[i - 1] = (bd[i - 1] + part[:, 2 * Z :]) * scale
            ysv[0, i - 1 : i, :] = value[0:1, :]
            ysv[1, i - 1 : i, :] = value[Y - 1 : Y, :]
            vin[0, i - 1 : i, :] = value[1:2, :]
            vin[1, i - 1 : i, :] = value[Y - 2 : Y - 1, :]
        visc[i] = value
    launch_down("yv")
    launch_up("yv")

    row_id = lax.broadcasted_iota(jnp.int32, (X, Z), 0)
    lane_id = lax.broadcasted_iota(jnp.int32, (1, Z), 1)
    first_row, last_row = row_id == 0, row_id == X - 1
    first_lane, last_lane = lane_id == 0, lane_id == Z - 1

    def y_next(plane):
        return pltpu.roll(plane, Y - 1, 0)

    def y_prev(plane):
        return pltpu.roll(plane, 1, 0)

    def x_next(plane, halo):
        return jnp.where(last_row, halo, pltpu.roll(plane, X - 1, 0))

    def x_prev(plane, halo):
        return jnp.where(first_row, halo, pltpu.roll(plane, 1, 0))

    def z_next(plane):
        return pltpu.roll(plane, Z - 1, 1)

    def z_prev(plane):
        return pltpu.roll(plane, 1, 1)

    def z_coefs(v):
        z_up = jnp.where(last_lane, 0.0, 0.5 * (v + z_next(v)))
        edge = jnp.where(first_lane | last_lane, 0.5 * v, 0.0)
        return z_up, z_prev(z_up), edge

    def update(coefs, scale, source, value, nexts, prevs, v):
        press = value[3]
        divergence = source[3]
        results = []
        for c in range(3):
            u = value[c]
            above = [nexts(c, d) for d in range(3)]
            below = [prevs(c, d) for d in range(3)]
            total = coefs[0] * above[0] + coefs[1] * below[0]
            total = total + coefs[2] * above[1] + coefs[3] * below[1]
            total = total + coefs[4] * above[2] + coefs[5] * below[2]
            ahead, behind = nexts(3, c), below[c]
            if c == 2:
                ahead = jnp.where(last_lane, 0.0, ahead)
                behind = jnp.where(first_lane, 0.0, behind)
            residual = source[c] + total - (ahead - press)
            results.append((1.0 - RELAX_VELOCITY) * u + scale * residual)
            divergence = divergence + (u - behind)
        results.append(press - RELAX_PRESSURE * v * divergence)
        return results

    def sweep(field, x):
        i = x + 1
        value = [field[c, i] for c in range(4)]

        def nexts(c, d):
            return (lambda: field[c, i + 1], lambda: y_next(value[c]), lambda: z_next(value[c]))[d]()

        def prevs(c, d):
            return (lambda: field[c, i - 1], lambda: y_prev(value[c]), lambda: z_prev(value[c]))[d]()

        coefs = (cx[i], cx[i - 1], cyu[x], cyl[x], czu[x], czl[x])
        source = [src[c, x] for c in range(4)]
        return update(coefs, rec[x], source, value, nexts, prevs, visc[i])

    def face_sweep(side, field, inner, outer, low_row, high_row):
        value = [field[side, c] for c in range(4)]

        def nexts(c, d):
            if d == 0:
                return x_next(value[c], high_row(c))
            if d == 1:
                return (inner if side == 0 else outer)[side, c]
            return z_next(value[c])

        def prevs(c, d):
            if d == 0:
                return x_prev(value[c], low_row(c))
            if d == 1:
                return (outer if side == 0 else inner)[side, c]
            return z_prev(value[c])

        coefs = [fc[side, k] for k in range(6)]
        source = [fsrc[side, c] for c in range(4)]
        return update(coefs, fc[side, 6], source, value, nexts, prevs, ysv[side])

    for i in range(X + 1):
        cx[i] = 0.5 * (visc[i] + visc[i + 1])
    arrive("x0")

    def first(x):
        v = visc[x + 1]
        y_up = 0.5 * (v + y_next(v))
        y_down = 0.5 * (v + y_prev(v))
        z_up, z_down, edge = z_coefs(v)
        cyu[x] = y_up
        cyl[x] = y_down
        czu[x] = z_up
        czl[x] = z_down
        rec[x] = RELAX_VELOCITY / (cx[x] + cx[x + 1] + y_up + y_down + z_up + z_down + edge)
        for c, plane in enumerate(sweep(f0, x)):
            f1[c, x + 1] = plane
            if x == 0:
                xs[0, c] = plane
            if x == X - 1:
                xs[1, c] = plane
            for side in range(2):
                row = inners[side]
                fin2[side, c, x : x + 1, :] = plane[row : row + 1, :]

    first(0)
    launch_down("x1")
    first(X - 1)
    launch_up("x1")
    for x in range(1, X - 1):
        first(x)

    arrive("y0")
    arrive("yv")
    for side in range(2):
        y = edges[side]
        v = ysv[side]
        above, below = (vin, yrv) if side == 0 else (yrv, vin)
        x_up = 0.5 * (v + x_next(v, visc[X + 1, y : y + 1, :]))
        x_down = 0.5 * (v + x_prev(v, visc[0, y : y + 1, :]))
        y_up = 0.5 * (v + above[side])
        y_down = 0.5 * (v + below[side])
        z_up, z_down, edge = z_coefs(v)
        total = x_up + x_down + y_up + y_down + z_up + z_down + edge
        for k, coef in enumerate((x_up, x_down, y_up, y_down, z_up, z_down)):
            fc[side, k] = coef
        fc[side, 6] = RELAX_VELOCITY / total
        planes = face_sweep(
            side,
            ys,
            fin,
            yr,
            lambda c: f0[c, 0, y : y + 1, :],
            lambda c: f0[c, X + 1, y : y + 1, :],
        )
        for c, plane in enumerate(planes):
            ys2[side, c] = plane
            xrs[0, side * 4 + c : side * 4 + c + 1, :] = plane[0:1, :]
            xrs[1, side * 4 + c : side * 4 + c + 1, :] = plane[X - 1 : X, :]
        if side == 0:
            launch_down("y1")
        else:
            launch_up("y1")
            launch_down("xr")
            launch_up("xr")
    for side in range(2):
        y = edges[side]
        for c in range(4):
            for x in range(X):
                f1[c, x + 1, y : y + 1, :] = ys2[side, c, x : x + 1, :]

    def second(x):
        planes = sweep(f1, x)
        for c, plane in enumerate(planes):
            out_ref[c, x] = plane
        sens_ref[x] = dens[x] * planes[2]

    for x in range(1, X - 1):
        second(x)
    arrive("x1")
    second(0)
    second(X - 1)

    arrive("y1")
    arrive("xr")
    for side in range(2):
        y = edges[side]
        planes = face_sweep(
            side,
            ys2,
            fin2,
            yr2,
            lambda c: xr[0, side * 4 + c : side * 4 + c + 1, :],
            lambda c: xr[1, side * 4 + c : side * 4 + c + 1, :],
        )
        for x in range(X):
            for c, plane in enumerate(planes):
                out_ref[c, x, y : y + 1, :] = plane[x : x + 1, :]
            sens_ref[x, y : y + 1, :] = dens[x, y : y + 1, :] * planes[2][x : x + 1, :]

    for copy in w_copies + m_copies:
        copy.wait_send()
    for name in pairs:
        sent(name)


def flush(end, sens, end_h, sens_h, sem):
    copies = [
        pltpu.make_async_copy(end.at[c], end_h.at[c], sem.at[c]) for c in range(end.shape[0])
    ]
    copies.append(pltpu.make_async_copy(sens, sens_h, sem.at[end.shape[0]]))
    for copy in copies:
        copy.start()
    for copy in copies:
        copy.wait()


def on_device(n, m, *arrays):
    start, weights = arrays[0], arrays[4]
    _, X, Y, Z = start.shape
    B = weights.shape[2]
    rows = n * B
    W = -(-rows // 128) * 128
    f32 = jnp.float32
    vmem = pl.BlockSpec(memory_space=pltpu.VMEM)
    hbm = pl.BlockSpec(memory_space=pltpu.HBM)
    block = pltpu.VMEM((X, Y, Z), f32)
    padded = pltpu.VMEM((X + 2, Y, Z), f32)
    faces = pltpu.VMEM((2, 4, X, Z), f32)
    face = pltpu.VMEM((2, X, Z), f32)
    dma = pltpu.SemaphoreType.DMA
    pinned = [
        array if array.ndim == 2 else pltpu.with_memory_space_constraint(array, pltpu.HBM)
        for array in arrays
    ]
    end, sens = pl.pallas_call(
        functools.partial(kernel, n, m),
        out_shape=(
            jax.ShapeDtypeStruct((4, X, Y, Z), f32),
            jax.ShapeDtypeStruct((X, Y, Z), f32),
        ),
        in_specs=[hbm] * 8 + [pl.BlockSpec(memory_space=pltpu.SMEM)] + [hbm] * 2,
        out_specs=(vmem, vmem),
        scratch_shapes=[
            pltpu.VMEM((4, X + 2, Y, Z), f32),
            pltpu.VMEM((4, X + 2, Y, Z), f32),
            pltpu.VMEM((4, X, Y, Z), f32),
            padded,
            block,
            padded,
            block,
            pltpu.VMEM((X + 1, Y, Z), f32),
            block,
            block,
            block,
            block,
            block,
            pltpu.VMEM(((X + 2) * Y, 3 * Z), f32),
            pltpu.VMEM((rows, Z), f32),
            pltpu.VMEM((8, W), f32),
            pltpu.VMEM((n, 8, W), f32),
            faces,
            faces,
            face,
            face,
            faces,
            faces,
            faces,
            faces,
            faces,
            face,
            pltpu.VMEM((2, 7, X, Z), f32),
            pltpu.VMEM((2, 4, Y, Z), f32),
            pltpu.VMEM((2, 8, Z), f32),
            pltpu.VMEM((2, 8, Z), f32),
            pltpu.VMEM((1, 1, B), jnp.int32),
            pltpu.VMEM((1, 1, B), jnp.int32),
            pltpu.VMEM((1, 1, B), jnp.int32),
            pltpu.SMEM(arrays[9].shape, f32),
            pltpu.SMEM(arrays[10].shape, f32),
            dma((10,)),
            dma((n,)),
            dma((n,)),
            dma((n,)),
            dma((n,)),
            dma((14,)),
            dma((14,)),
        ],
        compiler_params=pltpu.CompilerParams(
            collective_id=0, has_side_effects=True, vmem_limit_bytes=40 * 1024 * 1024
        ),
    )(*pinned)
    return pl.pallas_call(
        flush,
        out_shape=(
            jax.ShapeDtypeStruct(end.shape, f32),
            jax.ShapeDtypeStruct(sens.shape, f32),
        ),
        in_specs=[pl.BlockSpec(memory_space=pl.ANY)] * 2,
        out_specs=(hbm, hbm),
        compiler_params=pltpu.CompilerParams(vmem_limit_bytes=1024 * 1024),
        scratch_shapes=[dma((5,))],
    )(end, sens)


def solution(mesh):
    in_specs = (
        P(None, "gx", "gy", None),
        P(None, "gx", "gy", None),
        P("gx", "gy", None),
        P("gx", "gy", None),
        P("gx", "gy", None, None),
        P("gx", "gy", None),
        P("gx", "gy", None),
        P("gx", "gy", None),
        P("gx", "gy"),
        P(),
        P(),
    )
    out_specs = (P(None, "gx", "gy", None), P("gx", "gy", None))
    return jax.shard_map(
        functools.partial(on_device, mesh.shape["gx"], mesh.shape["gy"]),
        mesh=mesh,
        in_specs=in_specs,
        out_specs=out_specs,
        check_vma=False,
    )
```
